32 devices in a mesh: pipe: 16 (over z, y, core), ctx: 2 (over x).
Axes of the slice: x: 2, y: 2, z: 4, core: 2. Of those that a mesh axis runs over, the one named last changes fastest.
Arguments:
- query_fwd: bfloat16 [16, 256, 4096], P('pipe', 'ctx'), may hold values from -110 to 110
- key_fwd: bfloat16 [16, 256, 1024], P('pipe', 'ctx'), may hold values from -4.5 to 4.5
- value_fwd: bfloat16 [16, 256, 1024], P('pipe', 'ctx'), may hold values from -6 to 6
- query_bwd: bfloat16 [16, 256, 4096], P('pipe', 'ctx'), may hold values from -110 to 110
- key_bwd: bfloat16 [16, 256, 1024], P('pipe', 'ctx'), may hold values from -4.5 to 4.5
- value_bwd: bfloat16 [16, 256, 1024], P('pipe', 'ctx'), may hold values from -6 to 6
- cotangent: bfloat16 [16, 256, 4096], P('pipe', 'ctx'), may hold values from -6 to 6
- documents: int32 [16, 2, 256], P('pipe'), may hold values from 0 to 3, never falling along the last dimension, each value on 1 to 128 neighbouring positions
Outputs:
- attended: bfloat16 [16, 256, 4096], P('pipe', 'ctx')
- query_grad: bfloat16 [16, 256, 4096], P('pipe', 'ctx')
- key_grad: bfloat16 [16, 256, 1024], P('pipe', 'ctx')
- value_grad: bfloat16 [16, 256, 1024], P('pipe', 'ctx')
The draws below stay inside these ranges and needn't reach their ends.
Inputs may be any that keep to these rules, and one draw needn't show every extreme that they name: Along the last dimension ids never fall; 4 documents per slab, each of 1 to 128 positions, one of exactly 128.
All inputs are finite; a program needn't handle non-finite values.
Results may differ from the reference program's by a relative error of at most 0.0085.
Values may be sent and summed in bfloat16 or wider, within the bound.
A program may use at most 128 MiB of HBM per device.

```python
import math
import jax
import jax.numpy as jnp
import numpy as np
from jax import lax

QHEADS = 32
KVH = 8
HD = 128
QBLK = 128
DOCS = 4
SEQ = 256
SECTIONS = 16


def joint_draw(key, which):
    base = jax.random.fold_in(key, 101 + which)
    keys_drawn = jnp.clip(jax.random.normal(jax.random.fold_in(base, 1), (SECTIONS, SEQ, KVH, HD), jnp.float32), -4.0, 4.0)
    query_drawn = jnp.clip(jax.random.normal(jax.random.fold_in(base, 2), (SECTIONS, SEQ, KVH, QHEADS // KVH, HD), jnp.float32), -4.0, 4.0)
    return (query_drawn.reshape(SECTIONS, SEQ, QHEADS * HD), keys_drawn.reshape(SECTIONS, SEQ, KVH * HD))


def draw_query_fwd(key, part):
    return joint_draw(key, 0)[0].astype(jnp.bfloat16)


def draw_key_fwd(key, part):
    return joint_draw(key, 0)[1].astype(jnp.bfloat16)


def draw_query_bwd(key, part):
    return joint_draw(key, 1)[0].astype(jnp.bfloat16)


def draw_key_bwd(key, part):
    return joint_draw(key, 1)[1].astype(jnp.bfloat16)


def shard_levels(rng, dims, shards, smallest, high):
    level, own = 1.0, jax.random.fold_in(rng, 6)
    for dim, blocks in shards:
        steps = jnp.exp(jax.random.uniform(jax.random.fold_in(own, dim), (blocks,), jnp.float32, smallest / len(shards), high / len(shards)))
        level = level * jnp.repeat(steps, dims[dim] // blocks).reshape([-1 if axis == dim else 1 for axis in range(len(dims))])
    return level


def split_up(count, total, most, skew):
    portions = [(1 << 20) // math.isqrt(rank ** skew) + 1 for rank in range(2, count + 1)]
    rest, holding = total - most - (count - 1), [1] * (count - 1)
    while rest > 0:
        candidates = [i for i in range(count - 1) if holding[i] < most]
        pool, budget = sum([portions[i] for i in candidates]), rest
        for i in candidates:
            extra = min(most - holding[i], max(1, budget * portions[i] // pool), rest)
            holding[i] = holding[i] + extra
            rest = rest - extra
    return np.array([most] + holding)


def ragged_sizes(key, number_of, total, reach, slope):
    if number_of == 2:
        one = jax.random.randint(key, (), max(1, total - reach), min(reach, total - 1) + 1)
        return jnp.stack([one, total - one])
    lengths = jnp.asarray(split_up(number_of, total, reach, slope), jnp.int32)
    pairs = (number_of - 1) // 2
    donor, taker = lengths[1:1 + 2 * pairs:2], lengths[2:2 + 2 * pairs:2]
    margin = jnp.minimum(donor - 1, reach - taker)
    shifted = jax.random.randint(jax.random.fold_in(key, 1), (pairs,), 0, 1 << 20) % (margin + 1)
    lengths = lengths.at[1:1 + 2 * pairs:2].set(donor - shifted).at[2:2 + 2 * pairs:2].set(taker + shifted)
    return lengths[jax.random.permutation(jax.random.fold_in(key, 2), number_of)]


def bell_draw(key, shape, spread, reach, cuts=(), kind=jnp.bfloat16):
    result = jax.random.normal(key, shape, jnp.float32) * spread
    if len(cuts) > 0:
        result = shard_levels(key, shape, cuts, -0.22, 0.18) * result
    return jnp.clip(result, min=-reach, max=reach).astype(kind)


def setup_inputs(seed: int = 0) -> dict:
    seeds = jax.random.split(jax.random.key(seed), 9)
    return {
        "query_fwd": draw_query_fwd(jax.random.fold_in(seeds[8], 71), 0),
        "key_fwd": draw_key_fwd(jax.random.fold_in(seeds[8], 71), 0),
        "value_fwd": bell_draw(seeds[2], (SECTIONS, SEQ, KVH * HD), 1.0, 6.0, ((0, 16), (1, 2))),
        "query_bwd": draw_query_bwd(jax.random.fold_in(seeds[8], 71), 0),
        "key_bwd": draw_key_bwd(jax.random.fold_in(seeds[8], 71), 0),
        "value_bwd": bell_draw(seeds[5], (SECTIONS, SEQ, KVH * HD), 1.0, 6.0, ((0, 16), (1, 2))),
        "cotangent": bell_draw(seeds[6], (SECTIONS, SEQ, QHEADS * HD), 1.0, 6.0, ((0, 16), (1, 2))),
        "documents": jax.vmap(lambda own: jnp.searchsorted(jnp.cumsum(ragged_sizes(own, DOCS, SEQ, SEQ // 2, 1)), jnp.arange(SEQ), side="right"))(jax.random.split(seeds[7], SECTIONS * 2)).reshape((SECTIONS, 2, SEQ)).astype(jnp.int32),
    }


def allowed_mask(query_places, query_documents, key_places, key_documents):
    causal = key_places[None, :] <= query_places[:, None]
    same_document = key_documents[None, :] == query_documents[:, None]
    return causal & same_document


def head_probs(query_head, key_head, allowed, score_scale):
    raw_scores = jnp.einsum("rgd,kd->grk", query_head.astype(jnp.float32), key_head.astype(jnp.float32)) * score_scale
    masked = jnp.where(allowed[None], raw_scores, jnp.float32(-1e30))
    row_max = jnp.max(masked, axis=-1, keepdims=True)
    exponent = jnp.exp(masked - row_max)
    return exponent / jnp.sum(exponent, axis=-1, keepdims=True)


def forward_all(queries, keys_all, values_all, query_places, query_documents, key_places, key_documents):
    row_count, head_count, query_width = queries.shape
    head_size = keys_all.shape[2]
    score_scale = head_size ** -0.5
    block_count = row_count // QBLK
    query_blocks = queries.reshape(block_count, QBLK, head_count, query_width)
    place_blocks = query_places.reshape(block_count, QBLK)
    document_blocks = query_documents.reshape(block_count, QBLK)

    def one_block(packed):
        query_block, place_block, document_block = packed
        allowed = allowed_mask(place_block, document_block, key_places, key_documents)

        def one_head(head):
            query_head = lax.dynamic_index_in_dim(query_block, head, 1, False).reshape(QBLK, -1, head_size)
            key_head = lax.dynamic_index_in_dim(keys_all, head, 1, False)
            value_head = lax.dynamic_index_in_dim(values_all, head, 1, False)
            weights = head_probs(query_head, key_head, allowed, score_scale).astype(jnp.bfloat16)
            mixture = jnp.einsum("grk,kd->rgd", weights.astype(jnp.float32), value_head.astype(jnp.float32))
            return mixture.reshape(QBLK, query_width).astype(jnp.bfloat16)

        return jnp.moveaxis(lax.map(one_head, jnp.arange(head_count, dtype=jnp.int32)), 0, 1)

    outcome = lax.map(one_block, (query_blocks, place_blocks, document_blocks))
    return outcome.reshape(row_count, head_count, query_width)


def backward_all(queries, keys_all, values_all, cotan, query_places, query_documents, key_places, key_documents):
    row_count, head_count, query_width = queries.shape
    head_size = keys_all.shape[2]
    score_scale = head_size ** -0.5
    block_count = row_count // QBLK
    query_blocks = queries.reshape(block_count, QBLK, head_count, query_width)
    cotan_blocks = cotan.reshape(block_count, QBLK, head_count, query_width)
    place_blocks = query_places.reshape(block_count, QBLK)
    document_blocks = query_documents.reshape(block_count, QBLK)

    def one_block(totals, packed):
        query_block, cotan_block, place_block, document_block = packed
        allowed = allowed_mask(place_block, document_block, key_places, key_documents)

        def one_head(head):
            query_head = lax.dynamic_index_in_dim(query_block, head, 1, False).reshape(QBLK, -1, head_size)
            cotan_head = lax.dynamic_index_in_dim(cotan_block, head, 1, False).reshape(QBLK, -1, head_size)
            key_head = lax.dynamic_index_in_dim(keys_all, head, 1, False)
            value_head = lax.dynamic_index_in_dim(values_all, head, 1, False)
            probability = head_probs(query_head, key_head, allowed, score_scale)
            weights = probability.astype(jnp.bfloat16)
            prob_grad = jnp.einsum("rgd,kd->grk", cotan_head.astype(jnp.float32), value_head.astype(jnp.float32))
            row_delta = jnp.sum(probability * prob_grad, axis=-1, keepdims=True)
            score_grad = (probability * (prob_grad - row_delta) * score_scale).astype(jnp.bfloat16)
            query_part = jnp.einsum("grk,kd->rgd", score_grad.astype(jnp.float32), key_head.astype(jnp.float32))
            key_part = jnp.einsum("grk,rgd->kd", score_grad.astype(jnp.float32), query_head.astype(jnp.float32))
            value_part = jnp.einsum("grk,rgd->kd", weights.astype(jnp.float32), cotan_head.astype(jnp.float32))
            return query_part.reshape(QBLK, query_width).astype(jnp.bfloat16), key_part, value_part

        query_part, key_part, value_part = lax.map(one_head, jnp.arange(head_count, dtype=jnp.int32))
        new_totals = (totals[0] + jnp.moveaxis(key_part, 0, 1), totals[1] + jnp.moveaxis(value_part, 0, 1))
        return new_totals, jnp.moveaxis(query_part, 0, 1)

    empty_sum = jnp.zeros(keys_all.shape, jnp.float32)
    sums, query_grads = lax.scan(one_block, (empty_sum, empty_sum), (query_blocks, cotan_blocks, place_blocks, document_blocks))
    return query_grads.reshape(row_count, head_count, query_width), sums[0], sums[1]


def section_forward(packed):
    queries, keys_in, values_in, docs_row = packed
    places = jnp.arange(SEQ, dtype=jnp.int32)
    outcome = forward_all(queries.reshape(SEQ, KVH, -1), keys_in.reshape(SEQ, KVH, -1), values_in.reshape(SEQ, KVH, -1), places, docs_row, places, docs_row)
    return outcome.reshape(SEQ, -1)


def section_backward(packed):
    queries, keys_in, values_in, cotan, docs_row = packed
    places = jnp.arange(SEQ, dtype=jnp.int32)
    query_part, key_part, value_part = backward_all(queries.reshape(SEQ, KVH, -1), keys_in.reshape(SEQ, KVH, -1), values_in.reshape(SEQ, KVH, -1), cotan.reshape(SEQ, KVH, -1), places, docs_row, places, docs_row)
    return query_part.reshape(SEQ, -1), key_part.reshape(SEQ, -1).astype(jnp.bfloat16), value_part.reshape(SEQ, -1).astype(jnp.bfloat16)


def reference(query_fwd, key_fwd, value_fwd, query_bwd, key_bwd, value_bwd, cotangent, documents):
    attended = lax.map(section_forward, (jnp.roll(query_fwd, 1, 0), jnp.roll(key_fwd, 1, 0), jnp.roll(value_fwd, 1, 0), documents[:, 0]))
    query_part, key_part, value_part = lax.map(section_backward, (query_bwd, key_bwd, value_bwd, jnp.roll(cotangent, -1, 0), documents[:, 1]))
    return attended, jnp.roll(query_part, -1, 0), jnp.roll(key_part, -1, 0), jnp.roll(value_part, -1, 0)
```

```python
import functools
import math

import jax
import jax.numpy as jnp
from jax import lax
from jax.experimental import pallas as pl
from jax.experimental.pallas import tpu as pltpu
from jax.sharding import PartitionSpec as P

KVH = 8
F32 = jnp.float32
BF16 = jnp.bfloat16


def matmul(a, b, da, db):
    return lax.dot_general(a, b, (((da,), (db,)), ((), ())), preferred_element_type=F32)


def kernel(
    sections, shards, qf, kf, vf, qb, kb, vb, cot, docs, att_o, dq_o, dk_o, dv_o,
    qf_v, qb_v, g_v, kv, att_s, dq_s, dkv_s, dkv, part, docs_v, docs_r, bias,
    local_sem, docs_sem, kv_send, kv_recv, g_send, g_recv, part_send, part_recv,
    wide_send, wide_recv, dkv_send, dkv_recv,
):
    rows, width = qf.shape[1], qf.shape[2]
    narrow = kf.shape[2]
    hd = narrow // KVH
    group = width // narrow
    qw = group * hd
    scale = hd ** (-0.5)
    section, me = lax.axis_index("pipe"), lax.axis_index("ctx")
    after = lax.rem(section + 1, sections)
    before = lax.rem(section + sections - 1, sections)
    even = lax.rem(section, 2) == 0
    own = pl.ds(pl.multiple_of(me * rows, rows), rows)
    kv_in = (kf, vf, kb, vb)

    def remote(src, dst, send, recv, **where):
        return pltpu.make_async_remote_copy(
            src_ref=src, dst_ref=dst, send_sem=send, recv_sem=recv,
            device_id=where, device_id_type=pl.DeviceIdType.MESH,
        )

    def cols(c, size):
        return pl.ds(pl.multiple_of(c * size, size), size)

    def rows_of(j):
        return pl.ds(pl.multiple_of(j * rows, rows), rows)

    def docs_copy():
        return remote(docs.at[0], docs_r, docs_sem.at[0], docs_sem.at[1], pipe=before)

    def g_copy(c):
        at = cols(c, qw)
        return remote(cot.at[0, :, at], g_v.at[:, at], g_send.at[c], g_recv.at[c], pipe=before)

    def kv_copy(a, c, target, source):
        at = cols(c, hd)
        return remote(
            kv_in[a].at[0, :, at], kv.at[a, rows_of(source), at],
            kv_send.at[a, target, c], kv_recv.at[a, source, c], ctx=target,
        )

    def part_copy(a, c, target, source):
        at = cols(c, hd)
        return remote(
            dkv.at[a, rows_of(target), at], part.at[a, rows_of(source), at],
            part_send.at[a, target, c], part_recv.at[a, source, c], ctx=target,
        )

    def att_copy(c):
        at = cols(c, qw)
        return remote(
            att_s.at[:, at], att_o.at[0, :, at], wide_send.at[0, c], wide_recv.at[0, c], pipe=after
        )

    def dq_copy(c):
        at = cols(c, qw)
        return remote(
            dq_s.at[:, at], dq_o.at[0, :, at], wide_send.at[1, c], wide_recv.at[1, c], pipe=before
        )

    def dkv_copy(a, c):
        at = cols(c, hd)
        return remote(
            dkv_s.at[a, :, at], (dk_o, dv_o)[a].at[0, :, at],
            dkv_send.at[a, c], dkv_recv.at[a, c], pipe=before,
        )

    locals_ = [
        pltpu.make_async_copy(docs.at[0], docs_v, local_sem.at[0]),
        pltpu.make_async_copy(qf.at[0], qf_v, local_sem.at[1]),
        pltpu.make_async_copy(qb.at[0], qb_v, local_sem.at[2]),
    ] + [
        pltpu.make_async_copy(kv_in[a].at[0], kv.at[a, own], local_sem.at[3 + a]) for a in range(4)
    ]
    barrier = pltpu.get_barrier_semaphore()
    for where in (after, before):
        pl.semaphore_signal(
            barrier, inc=1, device_id={"pipe": where}, device_id_type=pl.DeviceIdType.MESH
        )
    for d in range(1, shards):
        pl.semaphore_signal(
            barrier, inc=1, device_id={"ctx": lax.rem(me + d, shards)},
            device_id_type=pl.DeviceIdType.MESH,
        )
    for copy in locals_:
        copy.start()
    for j in range(1, shards):

        @pl.when(j > me)
        def _():
            kv[:, j * rows : (j + 1) * rows, :] = jnp.zeros((4, rows, narrow), BF16)

    pl.semaphore_wait(barrier, shards + 1)
    docs_copy().start()

    def send_inputs(t, _):
        c = lax.rem(t, KVH)
        backward = (t < KVH) == even

        @pl.when(t < KVH)
        def _():
            g_copy(c).start()

        for j in range(1, shards):

            @pl.when(jnp.logical_and(j > me, backward))
            def _():
                kv_copy(2, c, j, me).start()
                kv_copy(3, c, j, me).start()

            @pl.when(jnp.logical_and(j > me, jnp.logical_not(backward)))
            def _():
                kv_copy(0, c, j, me).start()
                kv_copy(1, c, j, me).start()

        return 0

    lax.fori_loop(0, 2 * KVH, send_inputs, 0)
    for copy in locals_:
        copy.wait()
    docs_copy().wait_recv()

    for which, table in ((0, docs_r), (1, docs_v)):
        query_doc = table[which : which + 1, own].astype(F32)
        query_place = me * rows + lax.broadcasted_iota(jnp.int32, (rows, rows), 1)
        for j in range(shards):
            row = table[which : which + 1, j * rows : (j + 1) * rows].astype(F32)
            key_doc = jnp.transpose(jnp.broadcast_to(row, (rows, rows)))
            key_place = j * rows + lax.broadcasted_iota(jnp.int32, (rows, rows), 0)
            seen = jnp.logical_and(key_doc == query_doc, key_place <= query_place)
            bias[which, j * rows : (j + 1) * rows, :] = jnp.where(seen, F32(0), F32(-1e30))

    def stacked(ref, c):
        whole = ref[:, cols(c, qw)]
        return jnp.concatenate([whole[:, g * hd : (g + 1) * hd] for g in range(group)], axis=0)

    def probabilities(raw, which):
        masked = raw + bias[which]
        top = jnp.max(masked, axis=0, keepdims=True)
        power = jnp.exp2((masked - top) * F32(scale * math.log2(math.e)))
        return power * (F32(1) / jnp.sum(power, axis=0, keepdims=True))

    def forward(c):
        for j in range(shards - 1):

            @pl.when(j < me)
            def _():
                kv_copy(0, c, me, j).wait_recv()
                kv_copy(1, c, me, j).wait_recv()

        at = cols(c, hd)
        keys, values = kv[0, :, at], kv[1, :, at]
        raw = matmul(keys, stacked(qf_v, c), 1, 1)
        weights = jnp.concatenate(
            [
                probabilities(raw[:, g * rows : (g + 1) * rows], 0).astype(BF16)
                for g in range(group)
            ],
            axis=1,
        )
        mixed = matmul(weights, values, 0, 0)
        att_s[:, cols(c, qw)] = jnp.concatenate(
            [mixed[g * rows : (g + 1) * rows] for g in range(group)], axis=1
        ).astype(BF16)
        att_copy(c).start()

    def backward(c):
        for j in range(shards - 1):

            @pl.when(j < me)
            def _():
                kv_copy(2, c, me, j).wait_recv()
                kv_copy(3, c, me, j).wait_recv()

        g_copy(c).wait_recv()
        at = cols(c, hd)
        keys, values = kv[2, :, at], kv[3, :, at]
        queries, cotan = stacked(qb_v, c), stacked(g_v, c)
        raw = matmul(keys, queries, 1, 1)
        prob_grad = matmul(values, cotan, 1, 1)
        weights, score_grad = [], []
        for g in range(group):
            probs = probabilities(raw[:, g * rows : (g + 1) * rows], 1)
            grad = prob_grad[:, g * rows : (g + 1) * rows]
            delta = jnp.sum(probs * grad, axis=0, keepdims=True)
            weights.append(probs.astype(BF16))
            score_grad.append((probs * (grad - delta) * F32(scale)).astype(BF16))
        weights = jnp.concatenate(weights, axis=1)
        score_grad = jnp.concatenate(score_grad, axis=1)
        dq = matmul(score_grad, keys, 0, 0)
        dq_s[:, cols(c, qw)] = jnp.concatenate(
            [dq[g * rows : (g + 1) * rows] for g in range(group)], axis=1
        ).astype(BF16)
        dq_copy(c).start()
        dkv[0, :, at] = matmul(score_grad, queries, 1, 0)
        dkv[1, :, at] = matmul(weights, cotan, 1, 0)
        for j in range(shards - 1):

            @pl.when(j < me)
            def _():
                part_copy(0, c, j, me).start()
                part_copy(1, c, j, me).start()

    def step(t, _):
        c = lax.rem(t, KVH)
        is_backward = (t < KVH) == even
        pl.when(is_backward)(lambda: backward(c))
        pl.when(jnp.logical_not(is_backward))(lambda: forward(c))
        return 0

    lax.fori_loop(0, 2 * KVH, step, 0)

    def combine(c, _):
        at = cols(c, hd)
        for a in range(2):
            for j in range(1, shards):

                @pl.when(j > me)
                def _():
                    part_copy(a, c, me, j).wait_recv()
                    dkv[a, own, at] += part[a, j * rows : (j + 1) * rows, at]

            dkv_s[a, :, at] = dkv[a, own, at].astype(BF16)
            dkv_copy(a, c).start()
        return 0

    lax.fori_loop(0, KVH, combine, 0)

    docs_copy().wait_send()

    def finish(c, _):
        g_copy(c).wait_send()
        for a in range(4):
            for j in range(1, shards):
                pl.when(j > me)(lambda: kv_copy(a, c, j, me).wait_send())
        for a in range(2):
            for j in range(shards - 1):
                pl.when(j < me)(lambda: part_copy(a, c, j, me).wait_send())
        for copy in (att_copy(c), dq_copy(c), dkv_copy(0, c), dkv_copy(1, c)):
            copy.wait_send()
            copy.wait_recv()
        return 0

    lax.fori_loop(0, KVH, finish, 0)


def on_device(*args):
    query, key, documents = args[0], args[1], args[7]
    sections, shards = lax.axis_size("pipe"), lax.axis_size("ctx")
    rows, width = query.shape[1:]
    narrow = key.shape[2]
    seq = rows * shards
    dma = pltpu.SemaphoreType.DMA
    anywhere = pl.BlockSpec(memory_space=pl.ANY)
    return pl.pallas_call(
        functools.partial(kernel, sections, shards),
        name="relay_attention",
        out_shape=[
            jax.ShapeDtypeStruct(query.shape, BF16),
            jax.ShapeDtypeStruct(query.shape, BF16),
            jax.ShapeDtypeStruct(key.shape, BF16),
            jax.ShapeDtypeStruct(key.shape, BF16),
        ],
        in_specs=[anywhere] * 8,
        out_specs=[anywhere] * 4,
        scratch_shapes=[
            pltpu.VMEM((rows, width), BF16),
            pltpu.VMEM((rows, width), BF16),
            pltpu.VMEM((rows, width), BF16),
            pltpu.VMEM((4, seq, narrow), BF16),
            pltpu.VMEM((rows, width), BF16),
            pltpu.VMEM((rows, width), BF16),
            pltpu.VMEM((2, rows, narrow), BF16),
            pltpu.VMEM((2, seq, narrow), F32),
            pltpu.VMEM((2, seq, narrow), F32),
            pltpu.VMEM(documents.shape[1:], jnp.int32),
            pltpu.VMEM(documents.shape[1:], jnp.int32),
            pltpu.VMEM((2, seq, rows), F32),
            dma((7,)),
            dma((2,)),
            dma((4, shards, KVH)),
            dma((4, shards, KVH)),
            dma((KVH,)),
            dma((KVH,)),
            dma((2, shards, KVH)),
            dma((2, shards, KVH)),
            dma((2, KVH)),
            dma((2, KVH)),
            dma((2, KVH)),
            dma((2, KVH)),
        ],
        compiler_params=pltpu.CompilerParams(
            collective_id=0, has_side_effects=True, vmem_limit_bytes=56 * 2**20
        ),
    )(*args)


def solution(mesh):
    split = P("pipe", "ctx", None)
    return jax.shard_map(
        on_device,
        mesh=mesh,
        in_specs=(split,) * 7 + (P("pipe", None, None),),
        out_specs=(split,) * 4,
        check_vma=False,
    )
```

```python
import functools
import math

import jax
import jax.numpy as jnp
from jax import lax
from jax.experimental import pallas as pl
from jax.experimental.pallas import tpu as pltpu
from jax.sharding import PartitionSpec as P

KVH = 8
F32 = jnp.float32
BF16 = jnp.bfloat16


def matmul(a, b, da, db):
    return lax.dot_general(a, b, (((da,), (db,)), ((), ())), preferred_element_type=F32)


def kernel(
    sections, shards, qf, kf, vf, qb, kb, vb, cot, docs, att_o, dq_o, dk_o, dv_o,
    qf_v, qb_v, g_v, kv, att_s, dq_s, dkv_s, dkv, part, docs_v, docs_r, bias,
    local_sem, docs_sem, kv_send, kv_recv, g_send, g_recv, part_send, part_recv,
    wide_send, wide_recv, dkv_send, dkv_recv,
):
    rows, width = qf.shape[1], qf.shape[2]
    narrow = kf.shape[2]
    hd = narrow // KVH
    group = width // narrow
    qw = group * hd
    scale = hd ** (-0.5)
    section, me = lax.axis_index("pipe"), lax.axis_index("ctx")
    after = lax.rem(section + 1, sections)
    before = lax.rem(section + sections - 1, sections)
    even = lax.rem(section, 2) == 0
    own = pl.ds(pl.multiple_of(me * rows, rows), rows)
    kv_in = (kf, vf, kb, vb)

    def remote(src, dst, send, recv, **where):
        return pltpu.make_async_remote_copy(
            src_ref=src, dst_ref=dst, send_sem=send, recv_sem=recv,
            device_id=where, device_id_type=pl.DeviceIdType.MESH,
        )

    def cols(c, size):
        return pl.ds(pl.multiple_of(c * size, size), size)

    def rows_of(j):
        return pl.ds(pl.multiple_of(j * rows, rows), rows)

    def docs_copy():
        return remote(docs.at[0], docs_r, docs_sem.at[0], docs_sem.at[1], pipe=before)

    def g_copy(c):
        at = cols(c, qw)
        return remote(cot.at[0, :, at], g_v.at[:, at], g_send.at[c], g_recv.at[c], pipe=before)

    def kv_copy(a, c, target, source):
        at = cols(c, hd)
        return remote(
            kv_in[a].at[0, :, at], kv.at[a, rows_of(source), at],
            kv_send.at[a, target, c], kv_recv.at[a, source, c], ctx=target,
        )

    def part_copy(a, c, target, source):
        at = cols(c, hd)
        return remote(
            dkv.at[a, rows_of(target), at], part.at[a, rows_of(source), at],
            part_send.at[a, target, c], part_recv.at[a, source, c], ctx=target,
        )

    def att_copy(c):
        at = cols(c, qw)
        return remote(
            att_s.at[:, at], att_o.at[0, :, at], wide_send.at[0, c], wide_recv.at[0, c], pipe=after
        )

    def dq_copy(c):
        at = cols(c, qw)
        return remote(
            dq_s.at[:, at], dq_o.at[0, :, at], wide_send.at[1, c], wide_recv.at[1, c], pipe=before
        )

    def dkv_copy(a, c):
        at = cols(c, hd)
        return remote(
            dkv_s.at[a, :, at], (dk_o, dv_o)[a].at[0, :, at],
            dkv_send.at[a, c], dkv_recv.at[a, c], pipe=before,
        )

    locals_ = [
        pltpu.make_async_copy(docs.at[0], docs_v, local_sem.at[0]),
        pltpu.make_async_copy(qf.at[0], qf_v, local_sem.at[1]),
        pltpu.make_async_copy(qb.at[0], qb_v, local_sem.at[2]),
    ] + [
        pltpu.make_async_copy(kv_in[a].at[0], kv.at[a, own], local_sem.at[3 + a]) for a in range(4)
    ]
    barrier = pltpu.get_barrier_semaphore()
    for where in (after, before):
        pl.semaphore_signal(
            barrier, inc=1, device_id={"pipe": where}, device_id_type=pl.DeviceIdType.MESH
        )
    for d in range(1, shards):
        pl.semaphore_signal(
            barrier, inc=1, device_id={"ctx": lax.rem(me + d, shards)},
            device_id_type=pl.DeviceIdType.MESH,
        )
    for copy in locals_:
        copy.start()
    for j in range(1, shards):

        @pl.when(j > me)
        def _():
            kv[:, j * rows : (j + 1) * rows, :] = jnp.zeros((4, rows, narrow), BF16)

    pl.semaphore_wait(barrier, shards + 1)
    docs_copy().start()

    def send_inputs(t, _):
        c = lax.rem(t, KVH)
        backward = (t < KVH) == even

        @pl.when(t < KVH)
        def _():
            g_copy(c).start()

        for j in range(1, shards):

            @pl.when(jnp.logical_and(j > me, backward))
            def _():
                kv_copy(2, c, j, me).start()
                kv_copy(3, c, j, me).start()

            @pl.when(jnp.logical_and(j > me, jnp.logical_not(backward)))
            def _():
                kv_copy(0, c, j, me).start()
                kv_copy(1, c, j, me).start()

        return 0

    lax.fori_loop(0, 2 * KVH, send_inputs, 0)
    for copy in locals_:
        copy.wait()
    docs_copy().wait_recv()

    for which, table in ((0, docs_r), (1, docs_v)):
        query_doc = table[which : which + 1, own].astype(F32)
        query_place = me * rows + lax.broadcasted_iota(jnp.int32, (rows, rows), 1)
        for j in range(shards):
            row = table[which : which + 1, j * rows : (j + 1) * rows].astype(F32)
            key_doc = jnp.transpose(jnp.broadcast_to(row, (rows, rows)))
            key_place = j * rows + lax.broadcasted_iota(jnp.int32, (rows, rows), 0)
            seen = jnp.logical_and(key_doc == query_doc, key_place <= query_place)
            bias[which, j * rows : (j + 1) * rows, :] = jnp.where(seen, F32(0), F32(-1e30))

    def stacked(ref, c):
        whole = ref[:, cols(c, qw)]
        return jnp.concatenate([whole[:, g * hd : (g + 1) * hd] for g in range(group)], axis=0)

    def probabilities(raw, which):
        masked = raw + bias[which]
        top = jnp.max(masked, axis=0, keepdims=True)
        power = jnp.exp2((masked - top) * F32(scale * math.log2(math.e)))
        return power * (F32(1) / jnp.sum(power, axis=0, keepdims=True))

    def forward(c):
        for j in range(shards - 1):

            @pl.when(j < me)
            def _():
                kv_copy(0, c, me, j).wait_recv()
                kv_copy(1, c, me, j).wait_recv()

        at = cols(c, hd)
        keys, values = kv[0, :, at], kv[1, :, at]
        raw = matmul(keys, stacked(qf_v, c), 1, 1)
        weights = jnp.concatenate(
            [
                probabilities(raw[:, g * rows : (g + 1) * rows], 0).astype(BF16)
                for g in range(group)
            ],
            axis=1,
        )
        mixed = matmul(weights, values, 0, 0)
        att_s[:, cols(c, qw)] = jnp.concatenate(
            [mixed[g * rows : (g + 1) * rows] for g in range(group)], axis=1
        ).astype(BF16)
        att_copy(c).start()

    def backward(c):
        for j in range(shards - 1):

            @pl.when(j < me)
            def _():
                kv_copy(2, c, me, j).wait_recv()
                kv_copy(3, c, me, j).wait_recv()

        g_copy(c).wait_recv()
        at = cols(c, hd)
        keys, values = kv[2, :, at], kv[3, :, at]
        queries, cotan = stacked(qb_v, c), stacked(g_v, c)
        raw = matmul(keys, queries, 1, 1)
        prob_grad = matmul(values, cotan, 1, 1)
        weights, score_grad = [], []
        for g in range(group):
            probs = probabilities(raw[:, g * rows : (g + 1) * rows], 1)
            grad = prob_grad[:, g * rows : (g + 1) * rows]
            delta = jnp.sum(probs * grad, axis=0, keepdims=True)
            weights.append(probs.astype(BF16))
            score_grad.append((probs * (grad - delta) * F32(scale)).astype(BF16))
        weights = jnp.concatenate(weights, axis=1)
        score_grad = jnp.concatenate(score_grad, axis=1)
        dq = matmul(score_grad, keys, 0, 0)
        dq_s[:, cols(c, qw)] = jnp.concatenate(
            [dq[g * rows : (g + 1) * rows] for g in range(group)], axis=1
        ).astype(BF16)
        dq_copy(c).start()
        dkv[0, :, at] = matmul(score_grad, queries, 1, 0)
        dkv[1, :, at] = matmul(weights, cotan, 1, 0)
        for j in range(shards - 1):

            @pl.when(j < me)
            def _():
                part_copy(0, c, j, me).start()
                part_copy(1, c, j, me).start()

    def step(t, _):
        c = lax.rem(t, KVH)
        is_backward = (t < KVH) == even
        pl.when(is_backward)(lambda: backward(c))
        pl.when(jnp.logical_not(is_backward))(lambda: forward(c))
        return 0

    lax.fori_loop(0, 2 * KVH, step, 0)

    def combine(c, _):
        at = cols(c, hd)
        for a in range(2):
            for j in range(1, shards):

                @pl.when(j > me)
                def _():
                    part_copy(a, c, me, j).wait_recv()
                    dkv[a, own, at] += part[a, j * rows : (j + 1) * rows, at]

            dkv_s[a, :, at] = dkv[a, own, at].astype(BF16)
            dkv_copy(a, c).start()
        return 0

    lax.fori_loop(0, KVH, combine, 0)

    docs_copy().wait_send()

    def finish(c, _):
        g_copy(c).wait_send()
        for a in range(4):
            for j in range(1, shards):
                pl.when(j > me)(lambda: kv_copy(a, c, j, me).wait_send())
        for a in range(2):
            for j in range(shards - 1):
                pl.when(j < me)(lambda: part_copy(a, c, j, me).wait_send())
        for copy in (att_copy(c), dq_copy(c), dkv_copy(0, c), dkv_copy(1, c)):
            copy.wait_send()
            copy.wait_recv()
        return 0

    lax.fori_loop(0, KVH, finish, 0)


def store_kernel(*refs):
    half = len(refs) // 2
    sems = refs[-1]
    copies = [pltpu.make_async_copy(refs[i], refs[half + i], sems.at[i]) for i in range(half)]
    for copy in copies:
        copy.start()
    for copy in copies:
        copy.wait()


def stored(arrays):
    anywhere = pl.BlockSpec(memory_space=pl.ANY)
    return pl.pallas_call(
        store_kernel,
        name="store_outputs",
        out_shape=[pltpu.HBM(array.shape, array.dtype) for array in arrays],
        in_specs=[pl.BlockSpec(memory_space=pltpu.VMEM)] * len(arrays),
        out_specs=[anywhere] * len(arrays),
        scratch_shapes=[pltpu.SemaphoreType.DMA((len(arrays),))],
    )(*[pltpu.with_memory_space_constraint(array, pltpu.VMEM) for array in arrays])


def on_device(*args):
    query, key, documents = args[0], args[1], args[7]
    sections, shards = lax.axis_size("pipe"), lax.axis_size("ctx")
    rows, width = query.shape[1:]
    narrow = key.shape[2]
    seq = rows * shards
    dma = pltpu.SemaphoreType.DMA
    anywhere = pl.BlockSpec(memory_space=pl.ANY)
    return stored(pl.pallas_call(
        functools.partial(kernel, sections, shards),
        name="relay_attention",
        out_shape=[
            pltpu.VMEM(query.shape, BF16),
            pltpu.VMEM(query.shape, BF16),
            pltpu.VMEM(key.shape, BF16),
            pltpu.VMEM(key.shape, BF16),
        ],
        in_specs=[anywhere] * 8,
        out_specs=[pl.BlockSpec(memory_space=pltpu.VMEM)] * 4,
        scratch_shapes=[
            pltpu.VMEM((rows, width), BF16),
            pltpu.VMEM((rows, width), BF16),
            pltpu.VMEM((rows, width), BF16),
            pltpu.VMEM((4, seq, narrow), BF16),
            pltpu.VMEM((rows, width), BF16),
            pltpu.VMEM((rows, width), BF16),
            pltpu.VMEM((2, rows, narrow), BF16),
            pltpu.VMEM((2, seq, narrow), F32),
            pltpu.VMEM((2, seq, narrow), F32),
            pltpu.VMEM(documents.shape[1:], jnp.int32),
            pltpu.VMEM(documents.shape[1:], jnp.int32),
            pltpu.VMEM((2, seq, rows), F32),
            dma((7,)),
            dma((2,)),
            dma((4, shards, KVH)),
            dma((4, shards, KVH)),
            dma((KVH,)),
            dma((KVH,)),
            dma((2, shards, KVH)),
            dma((2, shards, KVH)),
            dma((2, KVH)),
            dma((2, KVH)),
            dma((2, KVH)),
            dma((2, KVH)),
        ],
        compiler_params=pltpu.CompilerParams(
            collective_id=0, has_side_effects=True, vmem_limit_bytes=56 * 2**20
        ),
    )(*args))


def solution(mesh):
    split = P("pipe", "ctx", None)
    return jax.shard_map(
        on_device,
        mesh=mesh,
        in_specs=(split,) * 7 + (P("pipe", None, None),),
        out_specs=(split,) * 4,
        check_vma=False,
    )
```

```python
import functools
import math

import jax
import jax.numpy as jnp
from jax import lax
from jax.experimental import pallas as pl
from jax.experimental.pallas import tpu as pltpu
from jax.sharding import PartitionSpec as P

KVH = 8
PIECES = 4
F32 = jnp.float32
BF16 = jnp.bfloat16


def matmul(a, b, da, db):
    return lax.dot_general(a, b, (((da,), (db,)), ((), ())), preferred_element_type=F32)


def kernel(
    sections, shards, qf, kf, vf, qb, kb, vb, cot, docs, att_o, dq_o, dk_o, dv_o,
    qf_v, qb_v, g_v, kv, att_s, dq_s, dkv_s, dkv, part, docs_v, docs_r, bias,
    local_sem, docs_sem, kv_send, kv_recv, g_send, g_recv, part_send, part_recv,
    wide_send, wide_recv, dkv_send, dkv_recv,
):
    rows, width = qf.shape[1], qf.shape[2]
    narrow = kf.shape[2]
    hd = narrow // KVH
    group = width // narrow
    qw = group * hd
    scale = hd ** (-0.5)
    section, me = lax.axis_index("pipe"), lax.axis_index("ctx")
    after = lax.rem(section + 1, sections)
    before = lax.rem(section + sections - 1, sections)
    even = lax.rem(section, 2) == 0
    own = pl.ds(pl.multiple_of(me * rows, rows), rows)
    kv_in = (kf, vf, kb, vb)

    def remote(src, dst, send, recv, **where):
        return pltpu.make_async_remote_copy(
            src_ref=src, dst_ref=dst, send_sem=send, recv_sem=recv,
            device_id=where, device_id_type=pl.DeviceIdType.MESH,
        )

    def cols(c, size):
        return pl.ds(pl.multiple_of(c * size, size), size)

    def rows_of(j):
        return pl.ds(pl.multiple_of(j * rows, rows), rows)

    def docs_copy():
        return remote(docs.at[0], docs_r, docs_sem.at[0], docs_sem.at[1], pipe=before)

    def g_copy(c):
        at = cols(c, qw)
        return remote(cot.at[0, :, at], g_v.at[:, at], g_send.at[c], g_recv.at[c], pipe=before)

    def kv_copy(a, c, target, source):
        at = cols(c, hd)
        return remote(
            kv_in[a].at[0, :, at], kv.at[a, rows_of(source), at],
            kv_send.at[a, target, c], kv_recv.at[a, source, c], ctx=target,
        )

    def part_copy(a, c, target, source):
        at = cols(c, hd)
        return remote(
            dkv.at[a, rows_of(target), at], part.at[a, rows_of(source), at],
            part_send.at[a, target, c], part_recv.at[a, source, c], ctx=target,
        )

    def att_copy(c):
        at = cols(c, qw)
        return remote(
            att_s.at[:, at], att_o.at[0, :, at], wide_send.at[0, c], wide_recv.at[0, c], pipe=after
        )

    def dq_copy(c):
        at = cols(c, qw)
        return remote(
            dq_s.at[:, at], dq_o.at[0, :, at], wide_send.at[1, c], wide_recv.at[1, c], pipe=before
        )

    def dkv_copy(a, c):
        at = cols(c, hd)
        return remote(
            dkv_s.at[a, :, at], (dk_o, dv_o)[a].at[0, :, at],
            dkv_send.at[a, c], dkv_recv.at[a, c], pipe=before,
        )

    locals_ = [
        pltpu.make_async_copy(docs.at[0], docs_v, local_sem.at[0]),
        pltpu.make_async_copy(qf.at[0], qf_v, local_sem.at[1]),
        pltpu.make_async_copy(qb.at[0], qb_v, local_sem.at[2]),
    ] + [
        pltpu.make_async_copy(kv_in[a].at[0], kv.at[a, own], local_sem.at[3 + a]) for a in range(4)
    ]
    barrier = pltpu.get_barrier_semaphore()
    for where in (after, before):
        pl.semaphore_signal(
            barrier, inc=1, device_id={"pipe": where}, device_id_type=pl.DeviceIdType.MESH
        )
    for d in range(1, shards):
        pl.semaphore_signal(
            barrier, inc=1, device_id={"ctx": lax.rem(me + d, shards)},
            device_id_type=pl.DeviceIdType.MESH,
        )
    for copy in locals_:
        copy.start()
    for j in range(1, shards):

        @pl.when(j > me)
        def _():
            kv[:, j * rows : (j + 1) * rows, :] = jnp.zeros((4, rows, narrow), BF16)

    pl.semaphore_wait(barrier, shards + 1)
    docs_copy().start()

    def send_inputs(t, _):
        c = lax.rem(t, KVH)
        backward = (t < KVH) == even

        @pl.when(t < KVH)
        def _():
            g_copy(c).start()

        for j in range(1, shards):

            @pl.when(jnp.logical_and(j > me, backward))
            def _():
                kv_copy(2, c, j, me).start()
                kv_copy(3, c, j, me).start()

            @pl.when(jnp.logical_and(j > me, jnp.logical_not(backward)))
            def _():
                kv_copy(0, c, j, me).start()
                kv_copy(1, c, j, me).start()

        return 0

    lax.fori_loop(0, 2 * KVH, send_inputs, 0)
    for copy in locals_:
        copy.wait()
    docs_copy().wait_recv()

    for which, table in ((0, docs_r), (1, docs_v)):
        query_doc = table[which : which + 1, own].astype(F32)
        query_place = me * rows + lax.broadcasted_iota(jnp.int32, (rows, rows), 1)
        for j in range(shards):
            row = table[which : which + 1, j * rows : (j + 1) * rows].astype(F32)
            key_doc = jnp.transpose(jnp.broadcast_to(row, (rows, rows)))
            key_place = j * rows + lax.broadcasted_iota(jnp.int32, (rows, rows), 0)
            seen = jnp.logical_and(key_doc == query_doc, key_place <= query_place)
            bias[which, j * rows : (j + 1) * rows, :] = jnp.where(seen, F32(0), F32(-1e30))

    def stacked(ref, c):
        whole = ref[:, cols(c, qw)]
        return jnp.concatenate([whole[:, g * hd : (g + 1) * hd] for g in range(group)], axis=0)

    def probabilities(raw, which):
        masked = raw + bias[which]
        top = jnp.max(masked, axis=0, keepdims=True)
        power = jnp.exp2((masked - top) * F32(scale * math.log2(math.e)))
        return power * (F32(1) / jnp.sum(power, axis=0, keepdims=True))

    def forward(c):
        for j in range(shards - 1):

            @pl.when(j < me)
            def _():
                kv_copy(0, c, me, j).wait_recv()
                kv_copy(1, c, me, j).wait_recv()

        at = cols(c, hd)
        keys, values = kv[0, :, at], kv[1, :, at]
        raw = matmul(keys, stacked(qf_v, c), 1, 1)
        weights = jnp.concatenate(
            [
                probabilities(raw[:, g * rows : (g + 1) * rows], 0).astype(BF16)
                for g in range(group)
            ],
            axis=1,
        )
        mixed = matmul(weights, values, 0, 0)
        att_s[:, cols(c, qw)] = jnp.concatenate(
            [mixed[g * rows : (g + 1) * rows] for g in range(group)], axis=1
        ).astype(BF16)
        att_copy(c).start()

    def backward(c):
        for j in range(shards - 1):

            @pl.when(j < me)
            def _():
                kv_copy(2, c, me, j).wait_recv()
                kv_copy(3, c, me, j).wait_recv()

        g_copy(c).wait_recv()
        at = cols(c, hd)
        keys, values = kv[2, :, at], kv[3, :, at]
        queries, cotan = stacked(qb_v, c), stacked(g_v, c)
        raw = matmul(keys, queries, 1, 1)
        prob_grad = matmul(values, cotan, 1, 1)
        weights, score_grad = [], []
        for g in range(group):
            probs = probabilities(raw[:, g * rows : (g + 1) * rows], 1)
            grad = prob_grad[:, g * rows : (g + 1) * rows]
            delta = jnp.sum(probs * grad, axis=0, keepdims=True)
            weights.append(probs.astype(BF16))
            score_grad.append((probs * (grad - delta) * F32(scale)).astype(BF16))
        weights = jnp.concatenate(weights, axis=1)
        score_grad = jnp.concatenate(score_grad, axis=1)
        dq = matmul(score_grad, keys, 0, 0)
        dq_s[:, cols(c, qw)] = jnp.concatenate(
            [dq[g * rows : (g + 1) * rows] for g in range(group)], axis=1
        ).astype(BF16)
        dq_copy(c).start()
        dkv[0, :, at] = matmul(score_grad, queries, 1, 0)
        dkv[1, :, at] = matmul(weights, cotan, 1, 0)
        for j in range(shards - 1):

            @pl.when(j < me)
            def _():
                part_copy(0, c, j, me).start()
                part_copy(1, c, j, me).start()

    def combine(c):
        at = cols(c, hd)
        for a in range(2):
            for j in range(1, shards):

                @pl.when(j > me)
                def _():
                    part_copy(a, c, me, j).wait_recv()
                    dkv[a, own, at] += part[a, j * rows : (j + 1) * rows, at]

            dkv_s[a, :, at] = dkv[a, own, at].astype(BF16)
            dkv_copy(a, c).start()

    def step(t, _):
        c = lax.rem(t, KVH)
        early, odd = t < KVH, jnp.logical_not(even)

        @pl.when(jnp.logical_and(t >= KVH, jnp.logical_or(even, t >= 2 * KVH)))
        def _():
            combine(c)

        pl.when(jnp.logical_and(t < 2 * KVH, early == even))(lambda: backward(c))
        pl.when(jnp.logical_and(t < 2 * KVH, early == odd))(lambda: forward(c))
        return 0

    lax.fori_loop(0, jnp.where(even, 2 * KVH, 3 * KVH), step, 0)

    docs_copy().wait_send()

    def finish(c, _):
        g_copy(c).wait_send()
        for a in range(4):
            for j in range(1, shards):
                pl.when(j > me)(lambda: kv_copy(a, c, j, me).wait_send())
        for a in range(2):
            for j in range(shards - 1):
                pl.when(j < me)(lambda: part_copy(a, c, j, me).wait_send())
        for copy in (att_copy(c), dq_copy(c), dkv_copy(0, c), dkv_copy(1, c)):
            copy.wait_send()
            copy.wait_recv()
        return 0

    lax.fori_loop(0, KVH, finish, 0)


def store_kernel(*refs):
    half = len(refs) // 2
    sems = refs[-1]
    copies = []
    for i in range(half):
        piece = refs[i].shape[1] // PIECES
        for k in range(PIECES):
            at = (0, slice(k * piece, (k + 1) * piece))
            copies.append(
                pltpu.make_async_copy(refs[i].at[at], refs[half + i].at[at], sems.at[i, k])
            )
    for copy in copies:
        copy.start()
    for copy in copies:
        copy.wait()


def stored(arrays):
    anywhere = pl.BlockSpec(memory_space=pl.ANY)
    return pl.pallas_call(
        store_kernel,
        name="store_outputs",
        out_shape=[pltpu.HBM(array.shape, array.dtype) for array in arrays],
        in_specs=[pl.BlockSpec(memory_space=pltpu.VMEM)] * len(arrays),
        out_specs=[anywhere] * len(arrays),
        scratch_shapes=[pltpu.SemaphoreType.DMA((len(arrays), PIECES))],
    )(*[pltpu.with_memory_space_constraint(array, pltpu.VMEM) for array in arrays])


def on_device(*args):
    query, key, documents = args[0], args[1], args[7]
    sections, shards = lax.axis_size("pipe"), lax.axis_size("ctx")
    rows, width = query.shape[1:]
    narrow = key.shape[2]
    seq = rows * shards
    dma = pltpu.SemaphoreType.DMA
    anywhere = pl.BlockSpec(memory_space=pl.ANY)
    return stored(pl.pallas_call(
        functools.partial(kernel, sections, shards),
        name="relay_attention",
        out_shape=[
            pltpu.VMEM(query.shape, BF16),
            pltpu.VMEM(query.shape, BF16),
            pltpu.VMEM(key.shape, BF16),
            pltpu.VMEM(key.shape, BF16),
        ],
        in_specs=[anywhere] * 8,
        out_specs=[pl.BlockSpec(memory_space=pltpu.VMEM)] * 4,
        scratch_shapes=[
            pltpu.VMEM((rows, width), BF16),
            pltpu.VMEM((rows, width), BF16),
            pltpu.VMEM((rows, width), BF16),
            pltpu.VMEM((4, seq, narrow), BF16),
            pltpu.VMEM((rows, width), BF16),
            pltpu.VMEM((rows, width), BF16),
            pltpu.VMEM((2, rows, narrow), BF16),
            pltpu.VMEM((2, seq, narrow), F32),
            pltpu.VMEM((2, seq, narrow), F32),
            pltpu.VMEM(documents.shape[1:], jnp.int32),
            pltpu.VMEM(documents.shape[1:], jnp.int32),
            pltpu.VMEM((2, seq, rows), F32),
            dma((7,)),
            dma((2,)),
            dma((4, shards, KVH)),
            dma((4, shards, KVH)),
            dma((KVH,)),
            dma((KVH,)),
            dma((2, shards, KVH)),
            dma((2, shards, KVH)),
            dma((2, KVH)),
            dma((2, KVH)),
            dma((2, KVH)),
            dma((2, KVH)),
        ],
        compiler_params=pltpu.CompilerParams(
            collective_id=0, has_side_effects=True, vmem_limit_bytes=56 * 2**20
        ),
    )(*args))


def solution(mesh):
    split = P("pipe", "ctx", None)
    return jax.shard_map(
        on_device,
        mesh=mesh,
        in_specs=(split,) * 7 + (P("pipe", None, None),),
        out_specs=(split,) * 4,
        check_vma=False,
    )
```

```python
import functools
import math

import jax
import jax.numpy as jnp
from jax import lax
from jax.experimental import pallas as pl
from jax.experimental.pallas import tpu as pltpu
from jax.sharding import PartitionSpec as P

KVH = 8
SPAN = 4
F32 = jnp.float32
BF16 = jnp.bfloat16


def matmul(a, b, da, db):
    return lax.dot_general(a, b, (((da,), (db,)), ((), ())), preferred_element_type=F32)


def kernel(
    sections, shards, qf, kf, vf, qb, kb, vb, cot, docs, att_o, dq_o, dk_o, dv_o,
    qf_v, qb_v, g_v, kv, att_s, dq_s, dkv_s, dkv, part, docs_v, docs_r, bias,
    local_sem, docs_sem, kv_send, kv_recv, g_send, g_recv, part_send, part_recv,
    wide_send, wide_recv, dkv_send, dkv_recv,
):
    rows, width = qf.shape[1], qf.shape[2]
    narrow = kf.shape[2]
    hd = narrow // KVH
    group = width // narrow
    qw = group * hd
    scale = hd ** (-0.5)
    section, me = lax.axis_index("pipe"), lax.axis_index("ctx")
    after = lax.rem(section + 1, sections)
    before = lax.rem(section + sections - 1, sections)
    even = lax.rem(section, 2) == 0
    own = pl.ds(pl.multiple_of(me * rows, rows), rows)
    kv_in = (kf, vf, kb, vb)

    def remote(src, dst, send, recv, **where):
        return pltpu.make_async_remote_copy(
            src_ref=src, dst_ref=dst, send_sem=send, recv_sem=recv,
            device_id=where, device_id_type=pl.DeviceIdType.MESH,
        )

    def cols(c, size):
        return pl.ds(pl.multiple_of(c * size, size), size)

    def rows_of(j):
        return pl.ds(pl.multiple_of(j * rows, rows), rows)

    def docs_copy():
        return remote(docs.at[0], docs_r, docs_sem.at[0], docs_sem.at[1], pipe=before)

    def g_copy(c):
        at = cols(c, qw)
        return remote(cot.at[0, :, at], g_v.at[:, at], g_send.at[c], g_recv.at[c], pipe=before)

    def kv_copy(a, c, target, source):
        at = cols(c, hd)
        return remote(
            kv_in[a].at[0, :, at], kv.at[a, rows_of(source), at],
            kv_send.at[a, target, c], kv_recv.at[a, source, c], ctx=target,
        )

    def part_copy(a, c, target, source):
        at = cols(c, hd)
        return remote(
            dkv.at[a, rows_of(target), at], part.at[a, rows_of(source), at],
            part_send.at[a, target, c], part_recv.at[a, source, c], ctx=target,
        )

    def att_copy(c):
        at = cols(c, qw)
        return remote(
            att_s.at[:, at], att_o.at[0, :, at], wide_send.at[0, c], wide_recv.at[0, c], pipe=after
        )

    def dq_copy(c):
        at = cols(c, qw)
        return remote(
            dq_s.at[:, at], dq_o.at[0, :, at], wide_send.at[1, c], wide_recv.at[1, c], pipe=before
        )

    def dkv_copy(a, c):
        at = cols(c, SPAN * hd)
        return remote(
            dkv_s.at[a, :, at], (dk_o, dv_o)[a].at[0, :, at],
            dkv_send.at[a, c], dkv_recv.at[a, c], pipe=before,
        )

    locals_ = [
        pltpu.make_async_copy(docs.at[0], docs_v, local_sem.at[0]),
        pltpu.make_async_copy(qf.at[0], qf_v, local_sem.at[1]),
        pltpu.make_async_copy(qb.at[0], qb_v, local_sem.at[2]),
    ] + [
        pltpu.make_async_copy(kv_in[a].at[0], kv.at[a, own], local_sem.at[3 + a]) for a in range(4)
    ]
    barrier = pltpu.get_barrier_semaphore()
    for where in (after, before):
        pl.semaphore_signal(
            barrier, inc=1, device_id={"pipe": where}, device_id_type=pl.DeviceIdType.MESH
        )
    for d in range(1, shards):
        pl.semaphore_signal(
            barrier, inc=1, device_id={"ctx": lax.rem(me + d, shards)},
            device_id_type=pl.DeviceIdType.MESH,
        )
    for copy in locals_:
        copy.start()
    for j in range(1, shards):

        @pl.when(j > me)
        def _():
            kv[:, j * rows : (j + 1) * rows, :] = jnp.zeros((4, rows, narrow), BF16)

    pl.semaphore_wait(barrier, shards + 1)
    docs_copy().start()

    def send_inputs(t, _):
        c = lax.rem(t, KVH)
        backward = (t < KVH) == even

        @pl.when(t < KVH)
        def _():
            g_copy(c).start()

        for j in range(1, shards):

            @pl.when(jnp.logical_and(j > me, backward))
            def _():
                kv_copy(2, c, j, me).start()
                kv_copy(3, c, j, me).start()

            @pl.when(jnp.logical_and(j > me, jnp.logical_not(backward)))
            def _():
                kv_copy(0, c, j, me).start()
                kv_copy(1, c, j, me).start()

        return 0

    lax.fori_loop(0, 2 * KVH, send_inputs, 0)
    for copy in locals_:
        copy.wait()
    docs_copy().wait_recv()

    for which, table in ((0, docs_r), (1, docs_v)):
        query_doc = table[which : which + 1, own].astype(F32)
        query_place = me * rows + lax.broadcasted_iota(jnp.int32, (rows, rows), 1)
        for j in range(shards):
            row = table[which : which + 1, j * rows : (j + 1) * rows].astype(F32)
            key_doc = jnp.transpose(jnp.broadcast_to(row, (rows, rows)))
            key_place = j * rows + lax.broadcasted_iota(jnp.int32, (rows, rows), 0)
            seen = jnp.logical_and(key_doc == query_doc, key_place <= query_place)
            bias[which, j * rows : (j + 1) * rows, :] = jnp.where(seen, F32(0), F32(-1e30))

    def stacked(ref, c):
        whole = ref[:, cols(c, qw)]
        return jnp.concatenate([whole[:, g * hd : (g + 1) * hd] for g in range(group)], axis=0)

    def probabilities(raw, which):
        masked = raw + bias[which]
        top = jnp.max(masked, axis=0, keepdims=True)
        power = jnp.exp2((masked - top) * F32(scale * math.log2(math.e)))
        return power * (F32(1) / jnp.sum(power, axis=0, keepdims=True))

    def forward(c):
        for j in range(shards - 1):

            @pl.when(j < me)
            def _():
                kv_copy(0, c, me, j).wait_recv()
                kv_copy(1, c, me, j).wait_recv()

        at = cols(c, hd)
        keys, values = kv[0, :, at], kv[1, :, at]
        raw = matmul(keys, stacked(qf_v, c), 1, 1)
        weights = jnp.concatenate(
            [
                probabilities(raw[:, g * rows : (g + 1) * rows], 0).astype(BF16)
                for g in range(group)
            ],
            axis=1,
        )
        mixed = matmul(weights, values, 0, 0)
        att_s[:, cols(c, qw)] = jnp.concatenate(
            [mixed[g * rows : (g + 1) * rows] for g in range(group)], axis=1
        ).astype(BF16)
        att_copy(c).start()

    def backward(c):
        for j in range(shards - 1):

            @pl.when(j < me)
            def _():
                kv_copy(2, c, me, j).wait_recv()
                kv_copy(3, c, me, j).wait_recv()

        g_copy(c).wait_recv()
        at = cols(c, hd)
        keys, values = kv[2, :, at], kv[3, :, at]
        queries, cotan = stacked(qb_v, c), stacked(g_v, c)
        raw = matmul(keys, queries, 1, 1)
        prob_grad = matmul(values, cotan, 1, 1)
        weights, score_grad = [], []
        for g in range(group):
            probs = probabilities(raw[:, g * rows : (g + 1) * rows], 1)
            grad = prob_grad[:, g * rows : (g + 1) * rows]
            delta = jnp.sum(probs * grad, axis=0, keepdims=True)
            weights.append(probs.astype(BF16))
            score_grad.append((probs * (grad - delta) * F32(scale)).astype(BF16))
        weights = jnp.concatenate(weights, axis=1)
        score_grad = jnp.concatenate(score_grad, axis=1)
        dq = matmul(score_grad, keys, 0, 0)
        dq_s[:, cols(c, qw)] = jnp.concatenate(
            [dq[g * rows : (g + 1) * rows] for g in range(group)], axis=1
        ).astype(BF16)
        dq_copy(c).start()
        dkv[0, :, at] = matmul(score_grad, queries, 1, 0)
        dkv[1, :, at] = matmul(weights, cotan, 1, 0)
        for j in range(shards - 1):

            @pl.when(j < me)
            def _():
                part_copy(0, c, j, me).start()
                part_copy(1, c, j, me).start()

    def combine(c):
        at = cols(c, hd)
        for a in range(2):
            for j in range(1, shards):

                @pl.when(j > me)
                def _():
                    part_copy(a, c, me, j).wait_recv()
                    dkv[a, own, at] += part[a, j * rows : (j + 1) * rows, at]

            dkv_s[a, :, at] = dkv[a, own, at].astype(BF16)

        @pl.when(lax.rem(c, SPAN) == SPAN - 1)
        def _():
            dkv_copy(0, lax.div(c, SPAN)).start()
            dkv_copy(1, lax.div(c, SPAN)).start()

    def step(t, _):
        c = lax.rem(t, KVH)
        early, odd = t < KVH, jnp.logical_not(even)

        @pl.when(jnp.logical_and(t >= KVH, jnp.logical_or(even, t >= 2 * KVH)))
        def _():
            combine(c)

        pl.when(jnp.logical_and(t < 2 * KVH, early == even))(lambda: backward(c))
        pl.when(jnp.logical_and(t < 2 * KVH, early == odd))(lambda: forward(c))
        return 0

    lax.fori_loop(0, jnp.where(even, 2 * KVH, 3 * KVH), step, 0)

    docs_copy().wait_send()

    def finish(c, _):
        g_copy(c).wait_send()
        for a in range(4):
            for j in range(1, shards):
                pl.when(j > me)(lambda: kv_copy(a, c, j, me).wait_send())
        for a in range(2):
            for j in range(shards - 1):
                pl.when(j < me)(lambda: part_copy(a, c, j, me).wait_send())
        for copy in (att_copy(c), dq_copy(c)):
            copy.wait_send()
            copy.wait_recv()
        return 0

    lax.fori_loop(0, KVH, finish, 0)
    for a in range(2):
        for c in range(KVH // SPAN):
            dkv_copy(a, c).wait_send()
            dkv_copy(a, c).wait_recv()


def store_kernel(*refs):
    half = len(refs) // 2
    sems = refs[-1]
    copies = [pltpu.make_async_copy(refs[i], refs[half + i], sems.at[i]) for i in range(half)]
    for copy in copies:
        copy.start()
    for copy in copies:
        copy.wait()


def stored(arrays):
    anywhere = pl.BlockSpec(memory_space=pl.ANY)
    return pl.pallas_call(
        store_kernel,
        name="store_outputs",
        out_shape=[pltpu.HBM(array.shape, array.dtype) for array in arrays],
        in_specs=[pl.BlockSpec(memory_space=pltpu.VMEM)] * len(arrays),
        out_specs=[anywhere] * len(arrays),
        scratch_shapes=[pltpu.SemaphoreType.DMA((len(arrays),))],
    )(*[pltpu.with_memory_space_constraint(array, pltpu.VMEM) for array in arrays])


def on_device(*args):
    query, key, documents = args[0], args[1], args[7]
    sections, shards = lax.axis_size("pipe"), lax.axis_size("ctx")
    rows, width = query.shape[1:]
    narrow = key.shape[2]
    seq = rows * shards
    dma = pltpu.SemaphoreType.DMA
    anywhere = pl.BlockSpec(memory_space=pl.ANY)
    return stored(pl.pallas_call(
        functools.partial(kernel, sections, shards),
        name="relay_attention",
        out_shape=[
            pltpu.VMEM(query.shape, BF16),
            pltpu.VMEM(query.shape, BF16),
            pltpu.VMEM(key.shape, BF16),
            pltpu.VMEM(key.shape, BF16),
        ],
        in_specs=[anywhere] * 8,
        out_specs=[pl.BlockSpec(memory_space=pltpu.VMEM)] * 4,
        scratch_shapes=[
            pltpu.VMEM((rows, width), BF16),
            pltpu.VMEM((rows, width), BF16),
            pltpu.VMEM((rows, width), BF16),
            pltpu.VMEM((4, seq, narrow), BF16),
            pltpu.VMEM((rows, width), BF16),
            pltpu.VMEM((rows, width), BF16),
            pltpu.VMEM((2, rows, narrow), BF16),
            pltpu.VMEM((2, seq, narrow), F32),
            pltpu.VMEM((2, seq, narrow), F32),
            pltpu.VMEM(documents.shape[1:], jnp.int32),
            pltpu.VMEM(documents.shape[1:], jnp.int32),
            pltpu.VMEM((2, seq, rows), F32),
            dma((7,)),
            dma((2,)),
            dma((4, shards, KVH)),
            dma((4, shards, KVH)),
            dma((KVH,)),
            dma((KVH,)),
            dma((2, shards, KVH)),
            dma((2, shards, KVH)),
            dma((2, KVH)),
            dma((2, KVH)),
            dma((2, KVH // SPAN)),
            dma((2, KVH // SPAN)),
        ],
        compiler_params=pltpu.CompilerParams(
            collective_id=0, has_side_effects=True, vmem_limit_bytes=56 * 2**20
        ),
    )(*args))


def solution(mesh):
    split = P("pipe", "ctx", None)
    return jax.shard_map(
        on_device,
        mesh=mesh,
        in_specs=(split,) * 7 + (P("pipe", None, None),),
        out_specs=(split,) * 4,
        check_vma=False,
    )
```

```python
import functools
import math

import jax
import jax.numpy as jnp
from jax import lax
from jax.experimental import pallas as pl
from jax.experimental.pallas import tpu as pltpu
from jax.sharding import PartitionSpec as P

KVH = 8
SPAN = 4
F32 = jnp.float32
BF16 = jnp.bfloat16


def matmul(a, b, da, db):
    return lax.dot_general(a, b, (((da,), (db,)), ((), ())), preferred_element_type=F32)


def kernel(
    sections, shards, qf, kf, vf, qb, kb, vb, cot, docs, att_o, dq_o, dk_o, dv_o,
    qf_v, qb_v, g_v, kv, att_s, dq_s, dkv_s, dkv, part, docs_v, docs_r, bias,
    local_sem, docs_sem, kv_send, kv_recv, g_send, g_recv, part_send, part_recv,
    wide_send, wide_recv, dkv_send, dkv_recv,
):
    rows, width = qf.shape[1], qf.shape[2]
    narrow = kf.shape[2]
    hd = narrow // KVH
    group = width // narrow
    qw = group * hd
    scale = hd ** (-0.5)
    section, me = lax.axis_index("pipe"), lax.axis_index("ctx")
    after = lax.rem(section + 1, sections)
    before = lax.rem(section + sections - 1, sections)
    even = lax.rem(section, 2) == 0
    own = pl.ds(pl.multiple_of(me * rows, rows), rows)
    kv_in = (kf, vf, kb, vb)

    def remote(src, dst, send, recv, **where):
        return pltpu.make_async_remote_copy(
            src_ref=src, dst_ref=dst, send_sem=send, recv_sem=recv,
            device_id=where, device_id_type=pl.DeviceIdType.MESH,
        )

    def cols(c, size):
        return pl.ds(pl.multiple_of(c * size, size), size)

    def rows_of(j):
        return pl.ds(pl.multiple_of(j * rows, rows), rows)

    def docs_copy():
        return remote(docs.at[0], docs_r, docs_sem.at[0], docs_sem.at[1], pipe=before)

    def g_copy(c):
        at = cols(c, qw)
        return remote(cot.at[0, :, at], g_v.at[:, at], g_send.at[c], g_recv.at[c], pipe=before)

    def kv_copy(a, c, target, source):
        at = cols(c, hd)
        return remote(
            kv_in[a].at[0, :, at], kv.at[a, rows_of(source), at],
            kv_send.at[a, target, c], kv_recv.at[a, source, c], ctx=target,
        )

    def part_copy(a, c, target, source):
        at = cols(c, hd)
        return remote(
            dkv.at[a, rows_of(target), at], part.at[a, rows_of(source), at],
            part_send.at[a, target, c], part_recv.at[a, source, c], ctx=target,
        )

    def att_copy(c):
        at = cols(c, qw)
        return remote(
            att_s.at[:, at], att_o.at[0, :, at], wide_send.at[0, c], wide_recv.at[0, c], pipe=after
        )

    def dq_copy(c):
        at = cols(c, qw)
        return remote(
            dq_s.at[:, at], dq_o.at[0, :, at], wide_send.at[1, c], wide_recv.at[1, c], pipe=before
        )

    def dkv_copy(a, c):
        at = cols(c, SPAN * hd)
        return remote(
            dkv_s.at[a, :, at], (dk_o, dv_o)[a].at[0, :, at],
            dkv_send.at[a, c], dkv_recv.at[a, c], pipe=before,
        )

    locals_ = [
        pltpu.make_async_copy(docs.at[0], docs_v, local_sem.at[0]),
        pltpu.make_async_copy(qf.at[0], qf_v, local_sem.at[1]),
        pltpu.make_async_copy(qb.at[0], qb_v, local_sem.at[2]),
    ] + [
        pltpu.make_async_copy(kv_in[a].at[0], kv.at[a, own], local_sem.at[3 + a]) for a in range(4)
    ]
    barrier = pltpu.get_barrier_semaphore()
    for where in (after, before):
        pl.semaphore_signal(
            barrier, inc=1, device_id={"pipe": where}, device_id_type=pl.DeviceIdType.MESH
        )
    for d in range(1, shards):
        pl.semaphore_signal(
            barrier, inc=1, device_id={"ctx": lax.rem(me + d, shards)},
            device_id_type=pl.DeviceIdType.MESH,
        )
    for copy in locals_:
        copy.start()
    for j in range(1, shards):

        @pl.when(j > me)
        def _():
            kv[:, j * rows : (j + 1) * rows, :] = jnp.zeros((4, rows, narrow), BF16)

    pl.semaphore_wait(barrier, shards + 1)
    for c in range(KVH):
        g_copy(c).start()
        if c == 0:
            docs_copy().start()

    def send_inputs(t, _):
        c = lax.rem(t, KVH)
        backward = (t < KVH) == even

        for j in range(1, shards):

            @pl.when(jnp.logical_and(j > me, backward))
            def _():
                kv_copy(2, c, j, me).start()
                kv_copy(3, c, j, me).start()

            @pl.when(jnp.logical_and(j > me, jnp.logical_not(backward)))
            def _():
                kv_copy(0, c, j, me).start()
                kv_copy(1, c, j, me).start()

        return 0

    lax.fori_loop(0, 2 * KVH, send_inputs, 0)
    for copy in locals_:
        copy.wait()
    docs_copy().wait_recv()

    for which, table in ((0, docs_r), (1, docs_v)):
        query_doc = table[which : which + 1, own].astype(F32)
        query_place = me * rows + lax.broadcasted_iota(jnp.int32, (rows, rows), 1)
        for j in range(shards):
            row = table[which : which + 1, j * rows : (j + 1) * rows].astype(F32)
            key_doc = jnp.transpose(jnp.broadcast_to(row, (rows, rows)))
            key_place = j * rows + lax.broadcasted_iota(jnp.int32, (rows, rows), 0)
            seen = jnp.logical_and(key_doc == query_doc, key_place <= query_place)
            bias[which, j * rows : (j + 1) * rows, :] = jnp.where(seen, F32(0), F32(-1e30))

    def stacked(ref, c):
        whole = ref[:, cols(c, qw)]
        return jnp.concatenate([whole[:, g * hd : (g + 1) * hd] for g in range(group)], axis=0)

    def probabilities(raw, which):
        masked = raw + bias[which]
        top = jnp.max(masked, axis=0, keepdims=True)
        power = jnp.exp2((masked - top) * F32(scale * math.log2(math.e)))
        return power * (F32(1) / jnp.sum(power, axis=0, keepdims=True))

    def forward(c):
        for j in range(shards - 1):

            @pl.when(j < me)
            def _():
                kv_copy(0, c, me, j).wait_recv()
                kv_copy(1, c, me, j).wait_recv()

        at = cols(c, hd)
        keys, values = kv[0, :, at], kv[1, :, at]
        raw = matmul(keys, stacked(qf_v, c), 1, 1)
        weights = jnp.concatenate(
            [
                probabilities(raw[:, g * rows : (g + 1) * rows], 0).astype(BF16)
                for g in range(group)
            ],
            axis=1,
        )
        mixed = matmul(weights, values, 0, 0)
        att_s[:, cols(c, qw)] = jnp.concatenate(
            [mixed[g * rows : (g + 1) * rows] for g in range(group)], axis=1
        ).astype(BF16)
        att_copy(c).start()

    def backward(c):
        for j in range(shards - 1):

            @pl.when(j < me)
            def _():
                kv_copy(2, c, me, j).wait_recv()
                kv_copy(3, c, me, j).wait_recv()

        g_copy(c).wait_recv()
        at = cols(c, hd)
        keys, values = kv[2, :, at], kv[3, :, at]
        queries, cotan = stacked(qb_v, c), stacked(g_v, c)
        raw = matmul(keys, queries, 1, 1)
        prob_grad = matmul(values, cotan, 1, 1)
        weights, score_grad = [], []
        for g in range(group):
            probs = probabilities(raw[:, g * rows : (g + 1) * rows], 1)
            grad = prob_grad[:, g * rows : (g + 1) * rows]
            delta = jnp.sum(probs * grad, axis=0, keepdims=True)
            weights.append(probs.astype(BF16))
            score_grad.append((probs * (grad - delta) * F32(scale)).astype(BF16))
        weights = jnp.concatenate(weights, axis=1)
        score_grad = jnp.concatenate(score_grad, axis=1)
        dq = matmul(score_grad, keys, 0, 0)
        dq_s[:, cols(c, qw)] = jnp.concatenate(
            [dq[g * rows : (g + 1) * rows] for g in range(group)], axis=1
        ).astype(BF16)
        dq_copy(c).start()
        dkv[0, :, at] = matmul(score_grad, queries, 1, 0)
        dkv[1, :, at] = matmul(weights, cotan, 1, 0)
        for j in range(shards - 1):

            @pl.when(j < me)
            def _():
                part_copy(0, c, j, me).start()
                part_copy(1, c, j, me).start()

    def combine(c):
        at = cols(c, hd)
        for a in range(2):
            for j in range(1, shards):

                @pl.when(j > me)
                def _():
                    part_copy(a, c, me, j).wait_recv()
                    dkv[a, own, at] += part[a, j * rows : (j + 1) * rows, at]

            dkv_s[a, :, at] = dkv[a, own, at].astype(BF16)

        @pl.when(lax.rem(c, SPAN) == SPAN - 1)
        def _():
            dkv_copy(0, lax.div(c, SPAN)).start()
            dkv_copy(1, lax.div(c, SPAN)).start()

    def step(t, _):
        c = lax.rem(t, KVH)
        early, odd = t < KVH, jnp.logical_not(even)

        @pl.when(jnp.logical_and(t >= KVH, jnp.logical_or(even, t >= 2 * KVH)))
        def _():
            combine(c)

        pl.when(jnp.logical_and(t < 2 * KVH, early == even))(lambda: backward(c))
        pl.when(jnp.logical_and(t < 2 * KVH, early == odd))(lambda: forward(c))
        return 0

    lax.fori_loop(0, jnp.where(even, 2 * KVH, 3 * KVH), step, 0)

    docs_copy().wait_send()

    def finish(c, _):
        g_copy(c).wait_send()
        for a in range(4):
            for j in range(1, shards):
                pl.when(j > me)(lambda: kv_copy(a, c, j, me).wait_send())
        for a in range(2):
            for j in range(shards - 1):
                pl.when(j < me)(lambda: part_copy(a, c, j, me).wait_send())
        for copy in (att_copy(c), dq_copy(c)):
            copy.wait_send()
            copy.wait_recv()
        return 0

    lax.fori_loop(0, KVH, finish, 0)
    for a in range(2):
        for c in range(KVH // SPAN):
            dkv_copy(a, c).wait_send()
            dkv_copy(a, c).wait_recv()


def store_kernel(*refs):
    half = len(refs) // 2
    sems = refs[-1]
    copies = [pltpu.make_async_copy(refs[i], refs[half + i], sems.at[i]) for i in range(half)]
    for copy in copies:
        copy.start()
    for copy in copies:
        copy.wait()


def stored(arrays):
    anywhere = pl.BlockSpec(memory_space=pl.ANY)
    return pl.pallas_call(
        store_kernel,
        name="store_outputs",
        out_shape=[pltpu.HBM(array.shape, array.dtype) for array in arrays],
        in_specs=[pl.BlockSpec(memory_space=pltpu.VMEM)] * len(arrays),
        out_specs=[anywhere] * len(arrays),
        scratch_shapes=[pltpu.SemaphoreType.DMA((len(arrays),))],
    )(*[pltpu.with_memory_space_constraint(array, pltpu.VMEM) for array in arrays])


def on_device(*args):
    query, key, documents = args[0], args[1], args[7]
    sections, shards = lax.axis_size("pipe"), lax.axis_size("ctx")
    rows, width = query.shape[1:]
    narrow = key.shape[2]
    seq = rows * shards
    dma = pltpu.SemaphoreType.DMA
    anywhere = pl.BlockSpec(memory_space=pl.ANY)
    return stored(pl.pallas_call(
        functools.partial(kernel, sections, shards),
        name="relay_attention",
        out_shape=[
            pltpu.VMEM(query.shape, BF16),
            pltpu.VMEM(query.shape, BF16),
            pltpu.VMEM(key.shape, BF16),
            pltpu.VMEM(key.shape, BF16),
        ],
        in_specs=[anywhere] * 8,
        out_specs=[pl.BlockSpec(memory_space=pltpu.VMEM)] * 4,
        scratch_shapes=[
            pltpu.VMEM((rows, width), BF16),
            pltpu.VMEM((rows, width), BF16),
            pltpu.VMEM((rows, width), BF16),
            pltpu.VMEM((4, seq, narrow), BF16),
            pltpu.VMEM((rows, width), BF16),
            pltpu.VMEM((rows, width), BF16),
            pltpu.VMEM((2, rows, narrow), BF16),
            pltpu.VMEM((2, seq, narrow), F32),
            pltpu.VMEM((2, seq, narrow), F32),
            pltpu.VMEM(documents.shape[1:], jnp.int32),
            pltpu.VMEM(documents.shape[1:], jnp.int32),
            pltpu.VMEM((2, seq, rows), F32),
            dma((7,)),
            dma((2,)),
            dma((4, shards, KVH)),
            dma((4, shards, KVH)),
            dma((KVH,)),
            dma((KVH,)),
            dma((2, shards, KVH)),
            dma((2, shards, KVH)),
            dma((2, KVH)),
            dma((2, KVH)),
            dma((2, KVH // SPAN)),
            dma((2, KVH // SPAN)),
        ],
        compiler_params=pltpu.CompilerParams(
            collective_id=0, has_side_effects=True, vmem_limit_bytes=56 * 2**20
        ),
    )(*args))


def solution(mesh):
    split = P("pipe", "ctx", None)
    return jax.shard_map(
        on_device,
        mesh=mesh,
        in_specs=(split,) * 7 + (P("pipe", None, None),),
        out_specs=(split,) * 4,
        check_vma=False,
    )
```
